512 devices in a mesh: leaf: 8 (over z), row: 8 (over y), col: 8 (over x, core).
Axes of the slice: x: 4, y: 8, z: 8, core: 2. Of those that a mesh axis runs over, the one named last changes fastest.
Arguments:
- child_inverse: bfloat16 [8, 2, 3072, 3072], P('leaf', None, 'row', 'col'), as said below
- child_rhs: bfloat16 [8, 2, 3072, 256], P('leaf', None, 'col'), may hold values from -6 to 6
- child_to_mid: bfloat16 [8, 2, 2048, 3072], P('leaf', None, ('row', 'col')), may hold values from -0.109375 to 0.109375
- child_to_root: bfloat16 [8, 2, 2048, 3072], P('leaf', None, ('row', 'col')), may hold values from -0.109375 to 0.109375
- mid_rows_list: int32 [8, 2, 2048], P('leaf'), may hold values from 0 to 4095, as said below
- root_rows_list: int32 [8, 2, 2048], P('leaf'), may hold values from 0 to 8191, as said below
- mid_inverse: bfloat16 [8, 4096, 4096], P('leaf', 'row', 'col'), as said below
- mid_rhs: bfloat16 [8, 4096, 256], P('leaf', 'col'), may hold values from -6 to 6
- mid_to_root: bfloat16 [8, 2048, 4096], P('leaf', ('row', 'col')), may hold values from -0.09375 to 0.09375
- mid_root_list: int32 [8, 2048], P('leaf'), may hold values from 0 to 8191, as said below
- root_inverse: bfloat16 [8192, 8192], P(('leaf', 'row'), 'col'), as said below
- root_rhs: bfloat16 [8192, 256], P('col'), may hold values from -6 to 6
Outputs:
- child_solution: bfloat16 [8, 2, 3072, 256], P('leaf', None, 'row')
- mid_solution: bfloat16 [8, 4096, 256], P('leaf', 'row')
- root_solution: bfloat16 [8192, 256], P(('leaf', 'row'))
The draws below stay inside these ranges and needn't reach their ends.
Inputs may be any that keep to these rules, and one draw needn't show every extreme that they name: `mid_rows_list`: each list of a child holds 2048 distinct rows of its middle supernode in increasing order, always with the first and the last. `root_rows_list`: each list of a child holds 2048 distinct rows of the root in increasing order, always with the first and the last. `mid_root_list`: each list holds 2048 distinct rows of the root in increasing order, always with the first and the last. `child_inverse`: lower triangular with a positive diagonal. `mid_inverse`: lower triangular with a positive diagonal. `root_inverse`: lower triangular with a positive diagonal.
All inputs are finite; a program needn't handle non-finite values.
Results may differ from the reference program's by a relative error of at most 0.0085.
Values may be sent and summed in bfloat16 or wider, within the bound.
A program may use at most 64 MiB of HBM per device.

```python
import math
import jax
import jax.numpy as jnp
from jax import lax

NRHS = 256
NCHILD = 2
CHILD_W = 3072
MID_W = 4096
ROOT_W = 8192
MID_ROWS = 2048
CROOT_ROWS = 2048
MROOT_ROWS = 2048
N_LEAF = 8


def lower_block(key, block_shape, block_order):
    row_ids = lax.broadcasted_iota(jnp.int32, block_shape, len(block_shape) - 2)
    column_ids = lax.broadcasted_iota(jnp.int32, block_shape, len(block_shape) - 1)
    key_lower, key_diagonal = jax.random.split(key)
    lower_part = jax.random.normal(key_lower, block_shape, jnp.float32)
    diagonal_part = jax.random.uniform(key_diagonal, block_shape, jnp.float32, 0.6, 1.4)
    spread_factor = 0.8 / math.sqrt(block_order)
    values = jnp.where(column_ids < row_ids, lower_part * spread_factor, jnp.where(column_ids == row_ids, diagonal_part, 0.0))
    return values.astype(jnp.bfloat16)


def row_subset(key, lead_shape, picked, width):
    full_shape = lead_shape + (width,)
    positions = lax.broadcasted_iota(jnp.int32, full_shape, len(lead_shape))
    scores = jax.random.randint(key, full_shape, 0, 131072) * width + positions
    scores = jnp.where(positions == 0, -2, jnp.where(positions == width - 1, -1, scores))
    chosen = jnp.argsort(scores, axis=-1)[..., :picked]
    return jnp.sort(chosen, axis=-1).astype(jnp.int32)


def draw_child_inverse(key, part):
    return lower_block(jax.random.fold_in(key, 11), (N_LEAF, NCHILD, CHILD_W, CHILD_W), CHILD_W)


def draw_mid_inverse(key, part):
    return lower_block(jax.random.fold_in(key, 12), (N_LEAF, MID_W, MID_W), MID_W)


def draw_root_inverse(key, part):
    return lower_block(jax.random.fold_in(key, 13), (ROOT_W, ROOT_W), ROOT_W)


def draw_mid_rows_list(key, part):
    return row_subset(jax.random.fold_in(key, 21), (N_LEAF, NCHILD), MID_ROWS, MID_W)


def draw_root_rows_list(key, part):
    return row_subset(jax.random.fold_in(key, 22), (N_LEAF, NCHILD), CROOT_ROWS, ROOT_W)


def draw_mid_root_list(key, part):
    return row_subset(jax.random.fold_in(key, 23), (N_LEAF,), MROOT_ROWS, ROOT_W)


def block_scale(own_key, shape, pieces, low, top_value):
    def one(position, blocks):
        draws = jax.random.uniform(jax.random.fold_in(jax.random.fold_in(own_key, 6), position), (blocks,), jnp.float32, low / len(pieces), top_value / len(pieces))
        return jnp.repeat(jnp.exp(draws), shape[position] // blocks).reshape((-1,) + (1,) * (len(shape) - position - 1))

    loudness = one(*pieces[0])
    for cut in pieces[1:]:
        loudness = loudness * one(*cut)
    return loudness


def centred(stream_key, dims, spread, limit, pieces=(), held_as=jnp.bfloat16):
    drawn = spread * jax.random.normal(stream_key, dims, jnp.float32)
    if pieces:
        drawn = drawn * block_scale(stream_key, dims, pieces, -0.22, 0.18)
    return jnp.clip(drawn, -limit, limit).astype(held_as)


def setup_inputs(seed: int = 0) -> dict:
    streams_of = jax.random.split(jax.random.key(seed), 13)
    child_inverse = draw_child_inverse(jax.random.fold_in(streams_of[12], 71), 0)
    child_rhs = centred(streams_of[1], (N_LEAF, NCHILD, CHILD_W, NRHS), 1.0, 6.0, ((0, 8), (2, 8)))
    child_to_mid = centred(streams_of[2], (N_LEAF, NCHILD, MID_ROWS, CHILD_W), CHILD_W ** -0.5, 0.109375, ((0, 8), (2, 64)))
    child_to_root = centred(streams_of[3], (N_LEAF, NCHILD, CROOT_ROWS, CHILD_W), CHILD_W ** -0.5, 0.109375, ((0, 8), (2, 64)))
    mid_rows_list = draw_mid_rows_list(jax.random.fold_in(streams_of[12], 71), 0)
    root_rows_list = draw_root_rows_list(jax.random.fold_in(streams_of[12], 71), 0)
    mid_inverse = draw_mid_inverse(jax.random.fold_in(streams_of[12], 71), 0)
    mid_rhs = centred(streams_of[7], (N_LEAF, MID_W, NRHS), 1.0, 6.0, ((0, 8), (1, 8)))
    mid_to_root = centred(streams_of[8], (N_LEAF, MROOT_ROWS, MID_W), MID_W ** -0.5, 0.09375, ((0, 8), (1, 64)))
    mid_root_list = draw_mid_root_list(jax.random.fold_in(streams_of[12], 71), 0)
    root_inverse = draw_root_inverse(jax.random.fold_in(streams_of[12], 71), 0)
    root_rhs = centred(streams_of[11], (ROOT_W, NRHS), 1.0, 6.0, ((0, 8),))
    return {"child_inverse": child_inverse, "child_rhs": child_rhs, "child_to_mid": child_to_mid, "child_to_root": child_to_root, "mid_rows_list": mid_rows_list, "root_rows_list": root_rows_list, "mid_inverse": mid_inverse, "mid_rhs": mid_rhs, "mid_to_root": mid_to_root, "mid_root_list": mid_root_list, "root_inverse": root_inverse, "root_rhs": root_rhs}


def scatter_rows(count, rows_list, values):
    width = values.shape[-1]
    flat_values = values.reshape(-1, width).astype(jnp.float32)
    return jnp.zeros((count, width), jnp.float32).at[rows_list.reshape(-1)].add(flat_values)


def mid_scatter(rows_list, values):
    return scatter_rows(MID_W, rows_list, values)


def reference(child_inverse, child_rhs, child_to_mid, child_to_root, mid_rows_list, root_rows_list, mid_inverse, mid_rhs, mid_to_root, mid_root_list, root_inverse, root_rhs):
    child_solution = jnp.einsum("gcij,gcjr->gcir", child_inverse.astype(jnp.float32), child_rhs.astype(jnp.float32)).astype(jnp.bfloat16)
    update_mid = jnp.einsum("gcuj,gcjr->gcur", child_to_mid.astype(jnp.float32), child_solution.astype(jnp.float32)).astype(jnp.bfloat16)
    update_root = jnp.einsum("gcuj,gcjr->gcur", child_to_root.astype(jnp.float32), child_solution.astype(jnp.float32)).astype(jnp.bfloat16)
    mid_terms = jax.vmap(mid_scatter)(mid_rows_list, update_mid)
    mid_input = (mid_rhs.astype(jnp.float32) - mid_terms).astype(jnp.bfloat16)
    mid_solution = jnp.einsum("gij,gjr->gir", mid_inverse.astype(jnp.float32), mid_input.astype(jnp.float32)).astype(jnp.bfloat16)
    update_top = jnp.einsum("guj,gjr->gur", mid_to_root.astype(jnp.float32), mid_solution.astype(jnp.float32)).astype(jnp.bfloat16)
    root_terms = scatter_rows(ROOT_W, root_rows_list, update_root) + scatter_rows(ROOT_W, mid_root_list, update_top)
    root_input = (root_rhs.astype(jnp.float32) - root_terms).astype(jnp.bfloat16)
    root_solution = jnp.dot(root_inverse, root_input, preferred_element_type=jnp.float32).astype(jnp.bfloat16)
    return child_solution, mid_solution, root_solution
```

```python
import functools

import jax
import jax.numpy as jnp
from jax import lax
from jax.experimental import pallas as pl
from jax.experimental.pallas import tpu as pltpu
from jax.sharding import PartitionSpec as P

MESH_ID = pl.DeviceIdType.MESH


def ring_hops(n, plus_longer):
    longer, shorter = n // 2, (n - 1) // 2
    return (longer, shorter) if plus_longer else (shorter, longer)


def arrivals(n):
    plus, minus = ring_hops(n, True)
    order = []
    for k in range(1, plus + 1):
        order.append((1, k))
        if k <= minus:
            order.append((-1, k))
    return order


def gather_kernel(first, second, paired, height, first_stride, second_stride, x_ref, o_ref, *sems):
    first_send, first_recv, second_send, second_recv, own_sem = sems[:5]
    mate_send, mate_recv = sems[5:] if paired else (None, None)
    n_first = lax.axis_size(first) if first else 1
    ways = 2 if paired else 1
    n_second = lax.axis_size(second) // ways
    me_first = lax.axis_index(first) if first else 0
    index = lax.axis_index(second)
    core = lax.rem(index, ways)
    me_second = lax.div(index, ways)
    mate = {second: me_second * ways + 1 - core}

    def first_peer(step):
        return {first: lax.rem(me_first + step + n_first, n_first)}

    def second_peer(step):
        return {second: lax.rem(me_second + step + n_second, n_second) * ways + core}

    def slot(a, b):
        row = pl.multiple_of(a * first_stride + b * second_stride, height)
        return o_ref.at[:, pl.ds(row, height), :]

    def at_first(step):
        return lax.rem(me_first + step + n_first, n_first) if n_first > 1 else me_first

    def at_second(step, side):
        return lax.rem(me_second + step + n_second, n_second) * ways + side

    greet = []
    if n_first > 1:
        greet += [first_peer(1)] + ([first_peer(-1)] if n_first > 2 else [])
    if n_second > 1:
        greet += [second_peer(1)] + ([second_peer(-1)] if n_second > 2 else [])
    if paired:
        greet += [mate]
    barrier = pltpu.get_barrier_semaphore()
    for peer in greet:
        pl.semaphore_signal(barrier, inc=1, device_id=peer, device_id_type=MESH_ID)
    pl.semaphore_wait(barrier, len(greet))

    started = []

    def send(src, dst, send_sem, recv_sem, peer):
        copy = pltpu.make_async_remote_copy(
            src_ref=src,
            dst_ref=dst,
            send_sem=send_sem,
            recv_sem=recv_sem,
            device_id=peer,
            device_id_type=MESH_ID,
        )
        copy.start()
        started.append(copy)

    def arrived(ref, send_sem, recv_sem, peer):
        pltpu.make_async_remote_copy(
            src_ref=ref,
            dst_ref=ref,
            send_sem=send_sem,
            recv_sem=recv_sem,
            device_id=peer,
            device_id_type=MESH_ID,
        ).wait_recv()

    order = arrivals(n_first)
    first_id = {key: i for i, key in enumerate(order)}
    second_id = {}
    for direction in (1, -1):
        for k in range(1, n_second // 2 + 1):
            second_id[direction, k] = len(second_id)
    n_ids = len(second_id)

    own = slot(me_first, index)
    keep = pltpu.make_async_copy(x_ref, own, own_sem)
    keep.start()

    def start_second(j, src, dst):
        hops = ring_hops(n_second, j % 2 == 0)
        for direction, limit in zip((1, -1), hops):
            if limit >= 1:
                i = second_id[direction, 1]
                send(src, dst, second_send.at[j, i], second_recv.at[j, i], second_peer(direction))
        if paired:
            send(src, dst, mate_send.at[j, n_ids], mate_recv.at[j, n_ids], mate)

    plus, minus = ring_hops(n_first, True)
    for direction, limit in ((1, plus), (-1, minus)):
        if limit >= 1:
            i = first_id[direction, 1]
            send(x_ref, own, first_send.at[i], first_recv.at[i], first_peer(direction))
    start_second(0, x_ref, own)

    depth = n_second // 2
    steps = [0] + [-d * k for d, k in order]
    for t in range(1, len(order) + 1 + depth):
        if t <= len(order):
            direction, k = order[t - 1]
            here = slot(at_first(steps[t]), index)
            i = first_id[direction, k]
            arrived(here, first_send.at[i], first_recv.at[i], first_peer(direction))
            if (direction, k + 1) in first_id:
                i = first_id[direction, k + 1]
                send(here, here, first_send.at[i], first_recv.at[i], first_peer(direction))
            start_second(t, here, here)
        for k in range(1, depth + 1):
            j = t - k
            if j < 0 or j > len(order):
                continue
            hops = ring_hops(n_second, j % 2 == 0)
            for direction, limit in zip((1, -1), hops):
                if k > limit:
                    continue
                here = slot(at_first(steps[j]), at_second(-direction * k, core))
                i = second_id[direction, k]
                arrived(here, second_send.at[j, i], second_recv.at[j, i], second_peer(direction))
                if k + 1 <= limit:
                    n = second_id[direction, k + 1]
                    send(
                        here,
                        here,
                        second_send.at[j, n],
                        second_recv.at[j, n],
                        second_peer(direction),
                    )
                if paired:
                    send(here, here, mate_send.at[j, i], mate_recv.at[j, i], mate)
    if paired:
        for j in range(len(order) + 1):
            here = slot(at_first(steps[j]), at_second(0, 1 - core))
            arrived(here, mate_send.at[j, n_ids], mate_recv.at[j, n_ids], mate)
            hops = ring_hops(n_second, j % 2 == 0)
            for direction, limit in zip((1, -1), hops):
                for k in range(1, limit + 1):
                    here = slot(at_first(steps[j]), at_second(-direction * k, 1 - core))
                    i = second_id[direction, k]
                    arrived(here, mate_send.at[j, i], mate_recv.at[j, i], mate)
    for copy in started:
        copy.wait_send()
    keep.wait()


def gather(x, first, second, paired, first_stride, second_stride, collective_id):
    lead, height, width = x.shape
    n_first = lax.axis_size(first) if first else 1
    n_devices = n_first * lax.axis_size(second)
    n_second = lax.axis_size(second) // (2 if paired else 1)
    n_ids = max(2 * (n_second // 2), 1)
    dma = pltpu.SemaphoreType.DMA
    scratch = [dma((max(n_first - 1, 1),))] * 2 + [dma((n_first, n_ids))] * 2 + [dma(())]
    if paired:
        scratch += [dma((n_first, n_ids + 1))] * 2
    body = functools.partial(
        gather_kernel, first, second, paired, height, first_stride, second_stride
    )
    return pl.pallas_call(
        body,
        out_shape=jax.ShapeDtypeStruct((lead, height * n_devices, width), x.dtype),
        in_specs=[pl.BlockSpec(memory_space=pltpu.VMEM)],
        out_specs=pl.BlockSpec(memory_space=pltpu.VMEM),
        scratch_shapes=scratch,
        compiler_params=pltpu.CompilerParams(collective_id=collective_id, has_side_effects=True),
    )(x)


def reduce_kernel(axis, x_ref, o_ref, held, send_sem, recv_sem):
    n = lax.axis_size(axis)
    me = lax.axis_index(axis)
    barrier = pltpu.get_barrier_semaphore()
    for d in range(1, n):
        pl.semaphore_signal(
            barrier, inc=1, device_id={axis: lax.rem(me + d, n)}, device_id_type=MESH_ID
        )
    pl.semaphore_wait(barrier, n - 1)
    copies = []
    for d in range(1, n):
        peer = lax.rem(me + d, n)
        copy = pltpu.make_async_remote_copy(
            src_ref=x_ref.at[peer],
            dst_ref=held.at[d - 1],
            send_sem=send_sem.at[d - 1],
            recv_sem=recv_sem.at[d - 1],
            device_id={axis: peer},
            device_id_type=MESH_ID,
        )
        copy.start()
        copies.append(copy)
    for copy in copies:
        copy.wait()
    total = x_ref[me].astype(jnp.float32)
    for d in range(1, n):
        total = total + held[d - 1].astype(jnp.float32)
    o_ref[...] = total.astype(o_ref.dtype)


def reduce_pieces(x, axis, out_dtype, collective_id):
    n, height, width = x.shape
    return pl.pallas_call(
        functools.partial(reduce_kernel, axis),
        out_shape=jax.ShapeDtypeStruct((height, width), out_dtype),
        in_specs=[pl.BlockSpec(memory_space=pltpu.VMEM)],
        out_specs=pl.BlockSpec(memory_space=pltpu.VMEM),
        scratch_shapes=[
            pltpu.VMEM((n - 1, height, width), x.dtype),
            pltpu.SemaphoreType.DMA((n - 1,)),
            pltpu.SemaphoreType.DMA((n - 1,)),
        ],
        compiler_params=pltpu.CompilerParams(collective_id=collective_id, has_side_effects=True),
    )(x)


def placed_sum(values, rows_list, start, count):
    flat = values.reshape(-1, values.shape[-1])
    offsets = rows_list.reshape(1, -1) - start
    picks = (offsets == lax.broadcasted_iota(jnp.int32, (count, 1), 0)).astype(jnp.bfloat16)
    return jnp.dot(picks, flat, preferred_element_type=jnp.float32)


def per_device(
    child_inverse,
    child_rhs,
    child_to_mid,
    child_to_root,
    mid_rows_list,
    root_rows_list,
    mid_inverse,
    mid_rhs,
    mid_to_root,
    mid_root_list,
    root_inverse,
    root_rhs,
):
    n_row, n_col, n_leaf = (lax.axis_size(name) for name in ("row", "col", "leaf"))
    row, col, leaf = (lax.axis_index(name) for name in ("row", "col", "leaf"))
    children, child_rows = child_inverse.shape[1], child_inverse.shape[2]
    width = child_rhs.shape[3]

    part = jnp.einsum(
        "cij,cjr->cir", child_inverse[0], child_rhs[0], preferred_element_type=jnp.float32
    ).astype(jnp.bfloat16)
    own_rows = child_rows // n_col
    part = part.reshape(children, n_col, own_rows, width).transpose(1, 0, 2, 3)
    solved = reduce_pieces(part.reshape(n_col, children * own_rows, width), "col", jnp.bfloat16, 0)
    child_whole = gather(
        solved.reshape(children, own_rows, width), "row", "col", True, child_rows, own_rows, 1
    )
    child_local = lax.dynamic_slice_in_dim(child_whole, row * child_rows, child_rows, 1)

    update_mid = jnp.einsum(
        "cuj,cjr->cur", child_to_mid[0], child_whole, preferred_element_type=jnp.float32
    ).astype(jnp.bfloat16)
    update_root = jnp.einsum(
        "cuj,cjr->cur", child_to_root[0], child_whole, preferred_element_type=jnp.float32
    ).astype(jnp.bfloat16)
    piece = update_mid.shape[1]
    updates = gather(
        jnp.concatenate((update_mid, update_root), axis=0), "row", "col", True, n_col * piece, piece, 2
    )

    mid_rows = mid_rhs.shape[1]
    mid_term = placed_sum(updates[:children], mid_rows_list, col * mid_rows, mid_rows)
    mid_input = (mid_rhs[0].astype(jnp.float32) - mid_term).astype(jnp.bfloat16)
    mid_part = jnp.dot(mid_inverse[0], mid_input, preferred_element_type=jnp.float32)
    mid_own = mid_inverse.shape[1] // n_col
    mid_solved = reduce_pieces(
        mid_part.astype(jnp.bfloat16).reshape(n_col, mid_own, width), "col", jnp.bfloat16, 3
    )
    mid_block = mid_inverse.shape[1]
    mid_whole = gather(mid_solved[None], "row", "col", True, mid_block, mid_own, 4)[0]
    mid_local = lax.dynamic_slice_in_dim(mid_whole, row * mid_block, mid_block, 0)

    update_top = jnp.dot(
        mid_to_root[0], mid_whole, preferred_element_type=jnp.float32
    ).astype(jnp.bfloat16)
    top_piece = update_top.shape[0]
    top = gather(update_top[None], "row", "col", True, n_col * top_piece, top_piece, 5)

    root_rows = root_rhs.shape[0]
    sub_rows = root_rows // n_row
    start = col * root_rows + row * sub_rows
    root_term = placed_sum(updates[children:], root_rows_list, start, sub_rows)
    root_term = root_term + placed_sum(top, mid_root_list, start, sub_rows)
    root_own = sub_rows // n_leaf
    root_sum = reduce_pieces(
        root_term.reshape(n_leaf, root_own, width), "leaf", jnp.float32, 6
    )
    own_rhs = lax.dynamic_slice_in_dim(root_rhs, row * sub_rows + leaf * root_own, root_own, 0)
    own_input = (own_rhs.astype(jnp.float32) - root_sum).astype(jnp.bfloat16)
    root_input = gather(own_input[None], "leaf", "row", False, root_own, sub_rows, 7)[0]
    root_part = jnp.dot(root_inverse, root_input, preferred_element_type=jnp.float32)
    out_own = root_part.shape[0] // n_col
    root_solved = reduce_pieces(
        root_part.reshape(n_col, out_own, width), "col", jnp.bfloat16, 8
    )
    root_solution = gather(root_solved[None], None, "col", True, 0, out_own, 9)[0]
    return (child_local[None], mid_local[None], root_solution)


def solution(mesh):
    in_specs = (
        P("leaf", None, "row", "col"),
        P("leaf", None, "col", None),
        P("leaf", None, ("row", "col"), None),
        P("leaf", None, ("row", "col"), None),
        P("leaf", None, None),
        P("leaf", None, None),
        P("leaf", "row", "col"),
        P("leaf", "col", None),
        P("leaf", ("row", "col"), None),
        P("leaf", None),
        P(("leaf", "row"), "col"),
        P("col", None),
    )
    out_specs = (P("leaf", None, "row", None), P("leaf", "row", None), P(("leaf", "row"), None))
    return jax.shard_map(
        per_device, mesh=mesh, in_specs=in_specs, out_specs=out_specs, check_vma=False
    )
```

```python
import functools

import jax
import jax.numpy as jnp
from jax import lax
from jax.experimental import pallas as pl
from jax.experimental.pallas import tpu as pltpu
from jax.sharding import PartitionSpec as P

MESH_ID = pl.DeviceIdType.MESH


def ring_hops(n, plus_longer):
    longer, shorter = n // 2, (n - 1) // 2
    return (longer, shorter) if plus_longer else (shorter, longer)


def spread_kernel(reduced, negated, first, second, paired, first_stride, second_stride, *refs):
    x_ref = refs[0]
    base_ref = refs[1] if negated else None
    o_ref = refs[1 + negated]
    scratch = refs[2 + negated :]
    first_send, first_recv, second_send, second_recv, mate_send, mate_recv, own_sem = scratch[:7]
    lead, height, width = x_ref.shape[-3:]
    n_first = lax.axis_size(first) if first else 1
    ways = 2 if paired else 1
    n_second = lax.axis_size(second) // ways
    relayed = n_second <= 4
    me_first = lax.axis_index(first) if first else 0
    index = lax.axis_index(second)
    core = lax.rem(index, ways)
    chip = lax.div(index, ways)
    mate = {second: chip * ways + 1 - core}

    def at_first(step):
        return lax.rem(me_first + step + n_first, n_first) if n_first > 1 else me_first

    def at_second(step, side):
        return lax.rem(chip + step + n_second, n_second) * ways + side

    def slot(a, b):
        row = pl.multiple_of(a * first_stride + b * second_stride, height)
        return o_ref.at[:, pl.ds(row, height), :]

    started = []

    def make(src, dst, send_sem, recv_sem, peer):
        return pltpu.make_async_remote_copy(
            src_ref=src,
            dst_ref=dst,
            send_sem=send_sem,
            recv_sem=recv_sem,
            device_id=peer,
            device_id_type=MESH_ID,
        )

    def send(*args):
        copy = make(*args)
        copy.start()
        started.append(copy)

    def arrived(ref, send_sem, recv_sem, peer):
        make(ref, ref, send_sem, recv_sem, peer).wait_recv()

    n_reduced = lax.axis_size(reduced) if reduced else 1
    me_reduced = lax.axis_index(reduced) if reduced else 0
    reduce_peers = [{reduced: lax.rem(me_reduced + d, n_reduced)} for d in range(1, n_reduced)]
    greet = list(reduce_peers)
    if reduced != first:
        greet += [{first: at_first(d)} for d in range(1, n_first)]
    if reduced != second:
        greet += [{second: at_second(d, core)} for d in range(1, n_second)]
        greet += [mate] if paired else []
    barrier = pltpu.get_barrier_semaphore()
    for peer in greet:
        pl.semaphore_signal(barrier, inc=1, device_id=peer, device_id_type=MESH_ID)
    pl.semaphore_wait(barrier, len(greet))

    own = slot(me_first, index)
    if reduced:
        held, reduce_send, reduce_recv = scratch[7:]
        pieces = []
        for d in sorted(range(1, n_reduced), key=lambda d: -min(d, n_reduced - d)):
            copy = make(
                x_ref.at[lax.rem(me_reduced + d, n_reduced)],
                held.at[d - 1],
                reduce_send.at[d - 1],
                reduce_recv.at[d - 1],
                reduce_peers[d - 1],
            )
            copy.start()
            pieces.append(copy)
        total = x_ref[me_reduced].astype(jnp.float32)
        for copy in pieces:
            copy.wait_recv()
        for d in range(1, n_reduced):
            total = total + held[d - 1].astype(jnp.float32)
        if negated:
            total = base_ref[...].astype(jnp.float32) - total
        own_row = pl.multiple_of(me_first * first_stride + index * second_stride, height)
        o_ref[:, pl.ds(own_row, height), :] = total.astype(o_ref.dtype)
        started.extend(pieces)
        src = own
    else:
        keep = pltpu.make_async_copy(x_ref, own, own_sem)
        keep.start()
        src = x_ref

    order = sorted(range(1, n_first), key=lambda d: min(d, n_first - d))
    for d in order:
        send(src, own, first_send.at[d - 1], first_recv.at[d - 1], {first: at_first(d)})

    far_first = sorted(range(1, n_second), key=lambda d: -min(d, n_second - d))

    def start_second(j, src, dst):
        if relayed:
            for direction, limit in zip((1, -1), ring_hops(n_second, j % 2 == 0)):
                if limit >= 1:
                    e = direction % n_second - 1
                    peer = {second: at_second(direction, core)}
                    send(src, dst, second_send.at[j, e], second_recv.at[j, e], peer)
        else:
            for d in far_first:
                peer = {second: at_second(d, core)}
                send(src, dst, second_send.at[j, d - 1], second_recv.at[j, d - 1], peer)
        if paired:
            send(src, dst, mate_send.at[j, 0], mate_recv.at[j, 0], mate)

    steps = [0] + order

    def take_second(j, direction, k, limit):
        d = direction * k % n_second
        here = slot(at_first(-steps[j]), at_second(-d, core))
        hop = direction if relayed else d
        peer = {second: at_second(hop, core)}
        arrived(here, second_send.at[j, d - 1], second_recv.at[j, d - 1], peer)
        if k + 1 <= limit:
            e = direction * (k + 1) % n_second - 1
            send(here, here, second_send.at[j, e], second_recv.at[j, e], peer)
        if paired:
            send(here, here, mate_send.at[j, d], mate_recv.at[j, d], mate)

    start_second(0, src, own)
    depth = n_second // 2 if relayed else 1
    lag = 1
    for t in range(1, n_first + lag + depth):
        if t < n_first:
            d = steps[t]
            here = slot(at_first(-d), index)
            arrived(here, first_send.at[d - 1], first_recv.at[d - 1], {first: at_first(d)})
            start_second(t, here, here)
        for k in range(1, depth + 1):
            j = t - lag - k + 1
            if j < 0 or j >= n_first:
                continue
            if relayed:
                for direction, limit in zip((1, -1), ring_hops(n_second, j % 2 == 0)):
                    if k <= limit:
                        take_second(j, direction, k, limit)
            else:
                for d in far_first[::-1]:
                    take_second(j, d, 1, 1)
    if paired:
        for j in range(n_first):
            for d in range(n_second):
                here = slot(at_first(-steps[j]), at_second(-d, 1 - core))
                arrived(here, mate_send.at[j, d], mate_recv.at[j, d], mate)
    for copy in started:
        copy.wait_send()
    if not reduced:
        keep.wait()


def spread(x, reduced, first, second, paired, first_stride, second_stride, collective_id, base=None):
    lead, height, width = x.shape[-3:]
    n_first = lax.axis_size(first) if first else 1
    n_devices = n_first * lax.axis_size(second)
    n_second = lax.axis_size(second) // (2 if paired else 1)
    dma = pltpu.SemaphoreType.DMA
    scratch = [dma((max(n_first - 1, 1),))] * 2 + [dma((n_first, max(n_second - 1, 1)))] * 2
    scratch += [dma((n_first, n_second))] * 2 + [dma(())]
    if reduced:
        n = x.shape[0] - 1
        scratch += [pltpu.VMEM((n,) + x.shape[1:], x.dtype), dma((n,)), dma((n,))]
    operands = (x,) if base is None else (x, base)
    body = functools.partial(
        spread_kernel, reduced, base is not None, first, second, paired, first_stride, second_stride
    )
    return pl.pallas_call(
        body,
        out_shape=jax.ShapeDtypeStruct((lead, height * n_devices, width), jnp.bfloat16),
        in_specs=[pl.BlockSpec(memory_space=pltpu.VMEM)] * len(operands),
        out_specs=pl.BlockSpec(memory_space=pltpu.VMEM),
        scratch_shapes=scratch,
        compiler_params=pltpu.CompilerParams(collective_id=collective_id, has_side_effects=True),
    )(*operands)


def placed_sum(values, rows_list, start, count):
    flat = values.reshape(-1, values.shape[-1])
    offsets = rows_list.reshape(1, -1) - start
    picks = (offsets == lax.broadcasted_iota(jnp.int32, (count, 1), 0)).astype(jnp.bfloat16)
    return jnp.dot(picks, flat, preferred_element_type=jnp.float32)


def per_device(
    child_inverse,
    child_rhs,
    child_to_mid,
    child_to_root,
    mid_rows_list,
    root_rows_list,
    mid_inverse,
    mid_rhs,
    mid_to_root,
    mid_root_list,
    root_inverse,
    root_rhs,
):
    n_row, n_col, n_leaf = (lax.axis_size(name) for name in ("row", "col", "leaf"))
    row, col, leaf = (lax.axis_index(name) for name in ("row", "col", "leaf"))
    children, child_rows = child_inverse.shape[1], child_inverse.shape[2]
    width = child_rhs.shape[3]

    part = jnp.einsum(
        "cij,cjr->cir", child_inverse[0], child_rhs[0], preferred_element_type=jnp.float32
    ).astype(jnp.bfloat16)
    own_rows = child_rows // n_col
    part = part.reshape(children, n_col, own_rows, width).transpose(1, 0, 2, 3)
    child_whole = spread(part, "col", "row", "col", True, child_rows, own_rows, 0)
    child_local = lax.dynamic_slice_in_dim(child_whole, row * child_rows, child_rows, 1)

    update_mid = jnp.einsum(
        "cuj,cjr->cur", child_to_mid[0], child_whole, preferred_element_type=jnp.float32
    ).astype(jnp.bfloat16)
    update_root = jnp.einsum(
        "cuj,cjr->cur", child_to_root[0], child_whole, preferred_element_type=jnp.float32
    ).astype(jnp.bfloat16)
    piece = update_mid.shape[1]
    stacked = jnp.concatenate((update_mid, update_root), axis=0)
    updates = spread(stacked, None, "row", "col", True, n_col * piece, piece, 1)

    mid_rows = mid_rhs.shape[1]
    mid_term = placed_sum(updates[:children], mid_rows_list, col * mid_rows, mid_rows)
    mid_input = (mid_rhs[0].astype(jnp.float32) - mid_term).astype(jnp.bfloat16)
    mid_part = jnp.dot(mid_inverse[0], mid_input, preferred_element_type=jnp.float32)
    mid_own = mid_inverse.shape[1] // n_col
    mid_block = mid_inverse.shape[1]
    mid_part = mid_part.astype(jnp.bfloat16).reshape(n_col, 1, mid_own, width)
    mid_whole = spread(mid_part, "col", "row", "col", True, mid_block, mid_own, 2)[0]
    mid_local = lax.dynamic_slice_in_dim(mid_whole, row * mid_block, mid_block, 0)

    update_top = jnp.dot(
        mid_to_root[0], mid_whole, preferred_element_type=jnp.float32
    ).astype(jnp.bfloat16)
    top_piece = update_top.shape[0]
    top = spread(update_top[None], None, "row", "col", True, n_col * top_piece, top_piece, 3)

    root_rows = root_rhs.shape[0]
    sub_rows = root_rows // n_row
    start = col * root_rows + row * sub_rows
    root_term = placed_sum(updates[children:], root_rows_list, start, sub_rows)
    root_term = root_term + placed_sum(top, mid_root_list, start, sub_rows)
    root_own = sub_rows // n_leaf
    own_rhs = lax.dynamic_slice_in_dim(root_rhs, row * sub_rows + leaf * root_own, root_own, 0)
    root_term = root_term.reshape(n_leaf, 1, root_own, width)
    root_input = spread(
        root_term, "leaf", "leaf", "row", False, root_own, sub_rows, 4, own_rhs[None]
    )[0]
    root_part = jnp.dot(root_inverse, root_input, preferred_element_type=jnp.float32)
    out_own = root_part.shape[0] // n_col
    root_part = root_part.reshape(n_col, 1, out_own, width)
    root_solution = spread(root_part, "col", None, "col", True, 0, out_own, 5)[0]
    return (child_local[None], mid_local[None], root_solution)


def solution(mesh):
    in_specs = (
        P("leaf", None, "row", "col"),
        P("leaf", None, "col", None),
        P("leaf", None, ("row", "col"), None),
        P("leaf", None, ("row", "col"), None),
        P("leaf", None, None),
        P("leaf", None, None),
        P("leaf", "row", "col"),
        P("leaf", "col", None),
        P("leaf", ("row", "col"), None),
        P("leaf", None),
        P(("leaf", "row"), "col"),
        P("col", None),
    )
    out_specs = (P("leaf", None, "row", None), P("leaf", "row", None), P(("leaf", "row"), None))
    return jax.shard_map(
        per_device, mesh=mesh, in_specs=in_specs, out_specs=out_specs, check_vma=False
    )
```

```python
import functools

import jax
import jax.numpy as jnp
from jax import lax
from jax.experimental import pallas as pl
from jax.experimental.pallas import tpu as pltpu
from jax.sharding import PartitionSpec as P

MESH_ID = pl.DeviceIdType.MESH
RELAY = False


def ring_hops(n, plus_longer):
    longer, shorter = n // 2, (n - 1) // 2
    return (longer, shorter) if plus_longer else (shorter, longer)


def spread_kernel(reduced, negated, first, second, paired, first_stride, second_stride, *refs):
    x_ref = refs[0]
    base_ref = refs[1] if negated else None
    o_ref = refs[1 + negated]
    scratch = refs[2 + negated :]
    first_send, first_recv, second_send, second_recv, mate_send, mate_recv, own_sem = scratch[:7]
    lead, height, width = x_ref.shape[-3:]
    n_first = lax.axis_size(first) if first else 1
    ways = 2 if paired else 1
    n_second = lax.axis_size(second) // ways
    relayed = RELAY and n_second <= 4
    me_first = lax.axis_index(first) if first else 0
    index = lax.axis_index(second)
    core = lax.rem(index, ways)
    chip = lax.div(index, ways)
    mate = {second: chip * ways + 1 - core}

    def at_first(step):
        return lax.rem(me_first + step + n_first, n_first) if n_first > 1 else me_first

    def at_second(step, side):
        return lax.rem(chip + step + n_second, n_second) * ways + side

    def slot(a, b):
        row = pl.multiple_of(a * first_stride + b * second_stride, height)
        return o_ref.at[:, pl.ds(row, height), :]

    started = []

    def make(src, dst, send_sem, recv_sem, peer):
        return pltpu.make_async_remote_copy(
            src_ref=src,
            dst_ref=dst,
            send_sem=send_sem,
            recv_sem=recv_sem,
            device_id=peer,
            device_id_type=MESH_ID,
        )

    def send(*args):
        copy = make(*args)
        copy.start()
        started.append(copy)

    def arrived(ref, send_sem, recv_sem, peer):
        make(ref, ref, send_sem, recv_sem, peer).wait_recv()

    n_reduced = lax.axis_size(reduced) if reduced else 1
    me_reduced = lax.axis_index(reduced) if reduced else 0
    reduce_peers = [{reduced: lax.rem(me_reduced + d, n_reduced)} for d in range(1, n_reduced)]
    greet = list(reduce_peers)
    if reduced != first:
        greet += [{first: at_first(d)} for d in range(1, n_first)]
    if reduced != second:
        greet += [{second: at_second(d, core)} for d in range(1, n_second)]
        greet += [mate] if paired else []
    barrier = pltpu.get_barrier_semaphore()
    for peer in greet:
        pl.semaphore_signal(barrier, inc=1, device_id=peer, device_id_type=MESH_ID)
    pl.semaphore_wait(barrier, len(greet))

    own = slot(me_first, index)
    if reduced:
        held, reduce_send, reduce_recv = scratch[7:]
        pieces = []
        for d in sorted(range(1, n_reduced), key=lambda d: -min(d, n_reduced - d)):
            copy = make(
                x_ref.at[lax.rem(me_reduced + d, n_reduced)],
                held.at[d - 1],
                reduce_send.at[d - 1],
                reduce_recv.at[d - 1],
                reduce_peers[d - 1],
            )
            copy.start()
            pieces.append(copy)
        total = x_ref[me_reduced].astype(jnp.float32)
        for copy in pieces:
            copy.wait_recv()
        for d in range(1, n_reduced):
            total = total + held[d - 1].astype(jnp.float32)
        if negated:
            total = base_ref[...].astype(jnp.float32) - total
        own_row = pl.multiple_of(me_first * first_stride + index * second_stride, height)
        o_ref[:, pl.ds(own_row, height), :] = total.astype(o_ref.dtype)
        started.extend(pieces)
        src = own
    else:
        keep = pltpu.make_async_copy(x_ref, own, own_sem)
        keep.start()
        src = x_ref

    order = sorted(range(1, n_first), key=lambda d: min(d, n_first - d))
    for d in order:
        send(src, own, first_send.at[d - 1], first_recv.at[d - 1], {first: at_first(d)})

    far_first = sorted(range(1, n_second), key=lambda d: -min(d, n_second - d))

    def start_second(j, src, dst):
        if relayed:
            for direction, limit in zip((1, -1), ring_hops(n_second, j % 2 == 0)):
                if limit >= 1:
                    e = direction % n_second - 1
                    peer = {second: at_second(direction, core)}
                    send(src, dst, second_send.at[j, e], second_recv.at[j, e], peer)
        else:
            for d in far_first:
                peer = {second: at_second(d, core)}
                send(src, dst, second_send.at[j, d - 1], second_recv.at[j, d - 1], peer)
        if paired:
            send(src, dst, mate_send.at[j, 0], mate_recv.at[j, 0], mate)

    steps = [0] + order

    def take_second(j, direction, k, limit):
        d = direction * k % n_second
        here = slot(at_first(-steps[j]), at_second(-d, core))
        hop = direction if relayed else d
        peer = {second: at_second(hop, core)}
        arrived(here, second_send.at[j, d - 1], second_recv.at[j, d - 1], peer)
        if k + 1 <= limit:
            e = direction * (k + 1) % n_second - 1
            send(here, here, second_send.at[j, e], second_recv.at[j, e], peer)
        if paired:
            send(here, here, mate_send.at[j, d], mate_recv.at[j, d], mate)

    start_second(0, src, own)
    for j in range(1, n_first):
        d = steps[j]
        here = slot(at_first(-d), index)
        arrived(here, first_send.at[d - 1], first_recv.at[d - 1], {first: at_first(d)})
        start_second(j, here, here)
    if relayed:
        for k in range(1, n_second // 2 + 1):
            for j in range(n_first):
                for direction, limit in zip((1, -1), ring_hops(n_second, j % 2 == 0)):
                    if k <= limit:
                        take_second(j, direction, k, limit)
    else:
        for j in range(n_first):
            for d in far_first[::-1]:
                take_second(j, d, 1, 1)
    if paired:
        for j in range(n_first):
            for d in range(n_second):
                here = slot(at_first(-steps[j]), at_second(-d, 1 - core))
                arrived(here, mate_send.at[j, d], mate_recv.at[j, d], mate)
    for copy in started:
        copy.wait_send()
    if not reduced:
        keep.wait()


def spread(x, reduced, first, second, paired, first_stride, second_stride, collective_id, base=None):
    lead, height, width = x.shape[-3:]
    n_first = lax.axis_size(first) if first else 1
    n_devices = n_first * lax.axis_size(second)
    n_second = lax.axis_size(second) // (2 if paired else 1)
    dma = pltpu.SemaphoreType.DMA
    scratch = [dma((max(n_first - 1, 1),))] * 2 + [dma((n_first, max(n_second - 1, 1)))] * 2
    scratch += [dma((n_first, n_second))] * 2 + [dma(())]
    if reduced:
        n = x.shape[0] - 1
        scratch += [pltpu.VMEM((n,) + x.shape[1:], x.dtype), dma((n,)), dma((n,))]
    operands = (x,) if base is None else (x, base)
    body = functools.partial(
        spread_kernel, reduced, base is not None, first, second, paired, first_stride, second_stride
    )
    return pl.pallas_call(
        body,
        out_shape=jax.ShapeDtypeStruct((lead, height * n_devices, width), jnp.bfloat16),
        in_specs=[pl.BlockSpec(memory_space=pltpu.VMEM)] * len(operands),
        out_specs=pl.BlockSpec(memory_space=pltpu.VMEM),
        scratch_shapes=scratch,
        compiler_params=pltpu.CompilerParams(collective_id=collective_id, has_side_effects=True),
    )(*operands)


def placed_sum(values, rows_list, start, count):
    flat = values.reshape(-1, values.shape[-1])
    offsets = rows_list.reshape(1, -1) - start
    picks = (offsets == lax.broadcasted_iota(jnp.int32, (count, 1), 0)).astype(jnp.bfloat16)
    return jnp.dot(picks, flat, preferred_element_type=jnp.float32)


def per_device(
    child_inverse,
    child_rhs,
    child_to_mid,
    child_to_root,
    mid_rows_list,
    root_rows_list,
    mid_inverse,
    mid_rhs,
    mid_to_root,
    mid_root_list,
    root_inverse,
    root_rhs,
):
    n_row, n_col, n_leaf = (lax.axis_size(name) for name in ("row", "col", "leaf"))
    row, col, leaf = (lax.axis_index(name) for name in ("row", "col", "leaf"))
    children, child_rows = child_inverse.shape[1], child_inverse.shape[2]
    width = child_rhs.shape[3]

    part = jnp.einsum(
        "cij,cjr->cir", child_inverse[0], child_rhs[0], preferred_element_type=jnp.float32
    ).astype(jnp.bfloat16)
    own_rows = child_rows // n_col
    part = part.reshape(children, n_col, own_rows, width).transpose(1, 0, 2, 3)
    child_whole = spread(part, "col", "row", "col", True, child_rows, own_rows, 0)
    child_local = lax.dynamic_slice_in_dim(child_whole, row * child_rows, child_rows, 1)

    update_mid = jnp.einsum(
        "cuj,cjr->cur", child_to_mid[0], child_whole, preferred_element_type=jnp.float32
    ).astype(jnp.bfloat16)
    update_root = jnp.einsum(
        "cuj,cjr->cur", child_to_root[0], child_whole, preferred_element_type=jnp.float32
    ).astype(jnp.bfloat16)
    piece = update_mid.shape[1]
    stacked = jnp.concatenate((update_mid, update_root), axis=0)
    updates = spread(stacked, None, "row", "col", True, n_col * piece, piece, 1)

    mid_rows = mid_rhs.shape[1]
    mid_term = placed_sum(updates[:children], mid_rows_list, col * mid_rows, mid_rows)
    mid_input = (mid_rhs[0].astype(jnp.float32) - mid_term).astype(jnp.bfloat16)
    mid_part = jnp.dot(mid_inverse[0], mid_input, preferred_element_type=jnp.float32)
    mid_own = mid_inverse.shape[1] // n_col
    mid_block = mid_inverse.shape[1]
    mid_part = mid_part.astype(jnp.bfloat16).reshape(n_col, 1, mid_own, width)
    mid_whole = spread(mid_part, "col", "row", "col", True, mid_block, mid_own, 2)[0]
    mid_local = lax.dynamic_slice_in_dim(mid_whole, row * mid_block, mid_block, 0)

    update_top = jnp.dot(
        mid_to_root[0], mid_whole, preferred_element_type=jnp.float32
    ).astype(jnp.bfloat16)
    top_piece = update_top.shape[0]
    top = spread(update_top[None], None, "row", "col", True, n_col * top_piece, top_piece, 3)

    root_rows = root_rhs.shape[0]
    sub_rows = root_rows // n_row
    start = col * root_rows + row * sub_rows
    root_term = placed_sum(updates[children:], root_rows_list, start, sub_rows)
    root_term = root_term + placed_sum(top, mid_root_list, start, sub_rows)
    root_own = sub_rows // n_leaf
    own_rhs = lax.dynamic_slice_in_dim(root_rhs, row * sub_rows + leaf * root_own, root_own, 0)
    root_term = root_term.reshape(n_leaf, 1, root_own, width)
    root_input = spread(
        root_term, "leaf", "row", "leaf", False, sub_rows, root_own, 4, own_rhs[None]
    )[0]
    root_part = jnp.dot(root_inverse, root_input, preferred_element_type=jnp.float32)
    out_own = root_part.shape[0] // n_col
    root_part = root_part.reshape(n_col, 1, out_own, width)
    root_solution = spread(root_part, "col", None, "col", True, 0, out_own, 5)[0]
    return (child_local[None], mid_local[None], root_solution)


def solution(mesh):
    in_specs = (
        P("leaf", None, "row", "col"),
        P("leaf", None, "col", None),
        P("leaf", None, ("row", "col"), None),
        P("leaf", None, ("row", "col"), None),
        P("leaf", None, None),
        P("leaf", None, None),
        P("leaf", "row", "col"),
        P("leaf", "col", None),
        P("leaf", ("row", "col"), None),
        P("leaf", None),
        P(("leaf", "row"), "col"),
        P("col", None),
    )
    out_specs = (P("leaf", None, "row", None), P("leaf", "row", None), P(("leaf", "row"), None))
    return jax.shard_map(
        per_device, mesh=mesh, in_specs=in_specs, out_specs=out_specs, check_vma=False
    )
```

```python
import functools

import jax
import jax.numpy as jnp
from jax import lax
from jax.experimental import pallas as pl
from jax.experimental.pallas import tpu as pltpu
from jax.sharding import PartitionSpec as P

MESH_ID = pl.DeviceIdType.MESH


def ring_hops(n, plus_longer):
    longer, shorter = n // 2, (n - 1) // 2
    return (longer, shorter) if plus_longer else (shorter, longer)


def spread_kernel(relayed, reduced, negated, first, second, paired, first_stride, second_stride, *refs):
    x_ref = refs[0]
    base_ref = refs[1] if negated else None
    o_ref = refs[1 + negated]
    scratch = refs[2 + negated :]
    first_send, first_recv, second_send, second_recv, mate_send, mate_recv, own_sem = scratch[:7]
    lead, height, width = x_ref.shape[-3:]
    n_first = lax.axis_size(first) if first else 1
    ways = 2 if paired else 1
    n_second = lax.axis_size(second) // ways
    me_first = lax.axis_index(first) if first else 0
    index = lax.axis_index(second)
    core = lax.rem(index, ways)
    chip = lax.div(index, ways)
    mate = {second: chip * ways + 1 - core}

    def at_first(step):
        return lax.rem(me_first + step + n_first, n_first) if n_first > 1 else me_first

    def at_second(step, side):
        return lax.rem(chip + step + n_second, n_second) * ways + side

    def slot(a, b):
        row = pl.multiple_of(a * first_stride + b * second_stride, height)
        return o_ref.at[:, pl.ds(row, height), :]

    started = []

    def make(src, dst, send_sem, recv_sem, peer):
        return pltpu.make_async_remote_copy(
            src_ref=src,
            dst_ref=dst,
            send_sem=send_sem,
            recv_sem=recv_sem,
            device_id=peer,
            device_id_type=MESH_ID,
        )

    def send(*args):
        copy = make(*args)
        copy.start()
        started.append(copy)

    def arrived(ref, send_sem, recv_sem, peer):
        make(ref, ref, send_sem, recv_sem, peer).wait_recv()

    n_reduced = lax.axis_size(reduced) if reduced else 1
    me_reduced = lax.axis_index(reduced) if reduced else 0
    reduce_peers = [{reduced: lax.rem(me_reduced + d, n_reduced)} for d in range(1, n_reduced)]
    greet = list(reduce_peers)
    if reduced != first:
        greet += [{first: at_first(d)} for d in range(1, n_first)]
    if reduced != second:
        greet += [{second: at_second(d, core)} for d in range(1, n_second)]
        greet += [mate] if paired else []
    barrier = pltpu.get_barrier_semaphore()
    for peer in greet:
        pl.semaphore_signal(barrier, inc=1, device_id=peer, device_id_type=MESH_ID)
    pl.semaphore_wait(barrier, len(greet))

    own = slot(me_first, index)
    if reduced:
        held, reduce_send, reduce_recv = scratch[7:]
        pieces = []
        for d in sorted(range(1, n_reduced), key=lambda d: -min(d, n_reduced - d)):
            copy = make(
                x_ref.at[lax.rem(me_reduced + d, n_reduced)],
                held.at[d - 1],
                reduce_send.at[d - 1],
                reduce_recv.at[d - 1],
                reduce_peers[d - 1],
            )
            copy.start()
            pieces.append(copy)
        total = x_ref[me_reduced].astype(jnp.float32)
        for copy in pieces:
            copy.wait_recv()
        for d in range(1, n_reduced):
            total = total + held[d - 1].astype(jnp.float32)
        if negated:
            total = base_ref[...].astype(jnp.float32) - total
        own_row = pl.multiple_of(me_first * first_stride + index * second_stride, height)
        o_ref[:, pl.ds(own_row, height), :] = total.astype(o_ref.dtype)
        started.extend(pieces)
        src = own
    else:
        keep = pltpu.make_async_copy(x_ref, own, own_sem)
        keep.start()
        src = x_ref

    order = sorted(range(1, n_first), key=lambda d: min(d, n_first - d))
    hybrid = relayed and n_first == 8
    for d in (1, 7, 2, 6) if hybrid else order:
        send(src, own, first_send.at[d - 1], first_recv.at[d - 1], {first: at_first(d)})

    far_first = sorted(range(1, n_second), key=lambda d: -min(d, n_second - d))

    def start_second(j, src, dst):
        if relayed:
            for direction, limit in zip((1, -1), ring_hops(n_second, j % 2 == 0)):
                if limit >= 1:
                    e = direction % n_second - 1
                    peer = {second: at_second(direction, core)}
                    send(src, dst, second_send.at[j, e], second_recv.at[j, e], peer)
        else:
            for d in far_first:
                peer = {second: at_second(d, core)}
                send(src, dst, second_send.at[j, d - 1], second_recv.at[j, d - 1], peer)
        if paired:
            send(src, dst, mate_send.at[j, 0], mate_recv.at[j, 0], mate)

    steps = [0] + order

    def take_second(j, direction, k, limit):
        d = direction * k % n_second
        here = slot(at_first(-steps[j]), at_second(-d, core))
        hop = direction if relayed else d
        peer = {second: at_second(hop, core)}
        arrived(here, second_send.at[j, d - 1], second_recv.at[j, d - 1], peer)
        if k + 1 <= limit:
            e = direction * (k + 1) % n_second - 1
            send(here, here, second_send.at[j, e], second_recv.at[j, e], peer)
        if paired:
            send(here, here, mate_send.at[j, d], mate_recv.at[j, d], mate)

    start_second(0, src, own)
    def take_first(j):
        d = steps[j]
        here = slot(at_first(-d), index)
        arrived(here, first_send.at[d - 1], first_recv.at[d - 1], {first: at_first(d)})
        if hybrid:
            for further in {2: (3, 4), 6: (5,)}.get(d, ()):
                send(
                    here,
                    here,
                    first_send.at[further - 1],
                    first_recv.at[further - 1],
                    {first: at_first(further - d)},
                )
        start_second(j, here, here)

    depth = n_second // 2

    def take_hop(j, k):
        if relayed:
            for direction, limit in zip((1, -1), ring_hops(n_second, j % 2 == 0)):
                if k <= limit:
                    take_second(j, direction, k, limit)
        else:
            for d in far_first[::-1]:
                if min(d, n_second - d) == k:
                    take_second(j, d, 1, 1)

    for j in range(1, n_first):
        take_first(j)
    for k in range(1, depth + 1):
        for j in range(n_first):
            take_hop(j, k)
    if paired:
        for j in range(n_first):
            for d in range(n_second):
                here = slot(at_first(-steps[j]), at_second(-d, 1 - core))
                arrived(here, mate_send.at[j, d], mate_recv.at[j, d], mate)
    for copy in started:
        copy.wait_send()
    if not reduced:
        keep.wait()


def spread(
    x,
    reduced,
    first,
    second,
    paired,
    first_stride,
    second_stride,
    collective_id,
    base=None,
    relayed=False,
):
    lead, height, width = x.shape[-3:]
    n_first = lax.axis_size(first) if first else 1
    n_devices = n_first * lax.axis_size(second)
    n_second = lax.axis_size(second) // (2 if paired else 1)
    dma = pltpu.SemaphoreType.DMA
    scratch = [dma((max(n_first - 1, 1),))] * 2 + [dma((n_first, max(n_second - 1, 1)))] * 2
    scratch += [dma((n_first, n_second))] * 2 + [dma(())]
    if reduced:
        n = x.shape[0] - 1
        scratch += [pltpu.VMEM((n,) + x.shape[1:], x.dtype), dma((n,)), dma((n,))]
    operands = (x,) if base is None else (x, base)
    body = functools.partial(
        spread_kernel,
        relayed,
        reduced,
        base is not None,
        first,
        second,
        paired,
        first_stride,
        second_stride,
    )
    return pl.pallas_call(
        body,
        out_shape=jax.ShapeDtypeStruct((lead, height * n_devices, width), jnp.bfloat16),
        in_specs=[pl.BlockSpec(memory_space=pltpu.VMEM)] * len(operands),
        out_specs=pl.BlockSpec(memory_space=pltpu.VMEM),
        scratch_shapes=scratch,
        compiler_params=pltpu.CompilerParams(collective_id=collective_id, has_side_effects=True),
    )(*operands)


def placed_sum(values, rows_list, start, count):
    flat = values.reshape(-1, values.shape[-1])
    offsets = rows_list.reshape(1, -1) - start
    picks = (offsets == lax.broadcasted_iota(jnp.int32, (count, 1), 0)).astype(jnp.bfloat16)
    return jnp.dot(picks, flat, preferred_element_type=jnp.float32)


def per_device(
    child_inverse,
    child_rhs,
    child_to_mid,
    child_to_root,
    mid_rows_list,
    root_rows_list,
    mid_inverse,
    mid_rhs,
    mid_to_root,
    mid_root_list,
    root_inverse,
    root_rhs,
):
    n_row, n_col, n_leaf = (lax.axis_size(name) for name in ("row", "col", "leaf"))
    row, col, leaf = (lax.axis_index(name) for name in ("row", "col", "leaf"))
    children, child_rows = child_inverse.shape[1], child_inverse.shape[2]
    width = child_rhs.shape[3]

    part = jnp.einsum(
        "cij,cjr->cir", child_inverse[0], child_rhs[0], preferred_element_type=jnp.float32
    ).astype(jnp.bfloat16)
    own_rows = child_rows // n_col
    part = part.reshape(children, n_col, own_rows, width).transpose(1, 0, 2, 3)
    child_whole = spread(
        part, "col", "row", "col", True, child_rows, own_rows, 0, relayed=True
    )
    child_local = lax.dynamic_slice_in_dim(child_whole, row * child_rows, child_rows, 1)

    update_mid = jnp.einsum(
        "cuj,cjr->cur", child_to_mid[0], child_whole, preferred_element_type=jnp.float32
    ).astype(jnp.bfloat16)
    update_root = jnp.einsum(
        "cuj,cjr->cur", child_to_root[0], child_whole, preferred_element_type=jnp.float32
    ).astype(jnp.bfloat16)
    piece = update_mid.shape[1]
    stacked = jnp.concatenate((update_mid, update_root), axis=0)
    updates = spread(
        stacked, None, "row", "col", True, n_col * piece, piece, 1, relayed=True
    )

    mid_rows = mid_rhs.shape[1]
    mid_term = placed_sum(updates[:children], mid_rows_list, col * mid_rows, mid_rows)
    mid_input = (mid_rhs[0].astype(jnp.float32) - mid_term).astype(jnp.bfloat16)
    mid_part = jnp.dot(mid_inverse[0], mid_input, preferred_element_type=jnp.float32)
    mid_own = mid_inverse.shape[1] // n_col
    mid_block = mid_inverse.shape[1]
    mid_part = mid_part.astype(jnp.bfloat16).reshape(n_col, 1, mid_own, width)
    mid_whole = spread(mid_part, "col", "row", "col", True, mid_block, mid_own, 2)[0]
    mid_local = lax.dynamic_slice_in_dim(mid_whole, row * mid_block, mid_block, 0)

    update_top = jnp.dot(
        mid_to_root[0], mid_whole, preferred_element_type=jnp.float32
    ).astype(jnp.bfloat16)
    top_piece = update_top.shape[0]
    top = spread(update_top[None], None, "row", "col", True, n_col * top_piece, top_piece, 3)

    root_rows = root_rhs.shape[0]
    sub_rows = root_rows // n_row
    start = col * root_rows + row * sub_rows
    root_term = placed_sum(updates[children:], root_rows_list, start, sub_rows)
    root_term = root_term + placed_sum(top, mid_root_list, start, sub_rows)
    root_own = sub_rows // n_leaf
    own_rhs = lax.dynamic_slice_in_dim(root_rhs, row * sub_rows + leaf * root_own, root_own, 0)
    root_term = root_term.reshape(n_leaf, 1, root_own, width)
    root_input = spread(
        root_term, "leaf", "row", "leaf", False, sub_rows, root_own, 4, own_rhs[None]
    )[0]
    root_part = jnp.dot(root_inverse, root_input, preferred_element_type=jnp.float32)
    out_own = root_part.shape[0] // n_col
    root_part = root_part.reshape(n_col, 1, out_own, width)
    root_solution = spread(root_part, "col", None, "col", True, 0, out_own, 5)[0]
    return (child_local[None], mid_local[None], root_solution)


def solution(mesh):
    in_specs = (
        P("leaf", None, "row", "col"),
        P("leaf", None, "col", None),
        P("leaf", None, ("row", "col"), None),
        P("leaf", None, ("row", "col"), None),
        P("leaf", None, None),
        P("leaf", None, None),
        P("leaf", "row", "col"),
        P("leaf", "col", None),
        P("leaf", ("row", "col"), None),
        P("leaf", None),
        P(("leaf", "row"), "col"),
        P("col", None),
    )
    out_specs = (P("leaf", None, "row", None), P("leaf", "row", None), P(("leaf", "row"), None))
    return jax.shard_map(
        per_device, mesh=mesh, in_specs=in_specs, out_specs=out_specs, check_vma=False
    )
```
